128 devices in a mesh: seq: 32 (over z, x, core), exp: 4 (over y).
Axes of the slice: x: 4, y: 4, z: 4, core: 2. Of those that a mesh axis runs over, the one named last changes fastest.
Arguments:
- queries: bfloat16 [4096, 5120], P('seq', 'exp'), may hold values from -48 to 48
- keys_values: bfloat16 [2, 4096, 1024], P(None, 'seq', 'exp'), may hold values from -8 to 8
- residual: bfloat16 [4096, 5120], P(('seq', 'exp')), may hold values from -6 to 6
- norm_gain: float32 [5120], replicated, may hold values from 0.1 to 1.9
- route_logit: float32 [4096], P(('seq', 'exp')), may hold values from -2 to -1
- expert_ids: int32 [4096, 1], P(('seq', 'exp')), may hold values from 0 to 3; in each aligned block of 32 rows (0 to 31, 32 to 63, ...) at most 12 rows name the same one
- out_weight: bfloat16 [5120, 5120], P('exp'), may hold values from -0.078125 to 0.078125
- gate_weight: bfloat16 [4, 5120, 8192], P('exp', None, 'seq'), may hold values from -0.25 to 0.25
- up_weight: bfloat16 [4, 5120, 8192], P('exp', None, 'seq'), may hold values from -0.25 to 0.25
- down_weight: bfloat16 [4, 8192, 5120], P('exp', 'seq'), may hold values from -0.125 to 0.125
Outputs:
- layer_output: bfloat16 [4096, 5120], P(('seq', 'exp'))
The draws below stay inside these ranges and needn't reach their ends.
Inputs may be any that keep to these rules, and one draw needn't show every extreme that they name: `expert_ids`: in each aligned block of 32 tokens (the tokens of one device) no expert is named more than 12 times, a bound that some block reaches.
All inputs are finite; a program needn't handle non-finite values.
Results may differ from the reference program's by a relative error of at most 0.015.
Values may be sent and summed in bfloat16 or wider, within the bound.
No kernel may reach another device: no remote copies, remote signals or barrier semaphores. Data moves between devices by JAX's collectives and lax.ppermute only.
A program may use at most 128 MiB of HBM per device.

```python
import math
import jax
import jax.numpy as jnp
import numpy as np
from jax import lax

D = 5120
H = 40
KVH = 8
HD = 128
FF = 8192
TOKENS = 4096
SPAN = 4096
TOK_DEV = 32
EXPERTS = 4
CAP = 12
FF_DEV = 256


def attention_draw(key):
    base_key = jax.random.fold_in(key, 7)
    query_key, key_key, value_key = jax.random.split(base_key, 3)
    queries = jax.random.truncated_normal(query_key, -4.0, 4.0, (TOKENS, H * HD), jnp.float32) * 3.0
    keys = jax.random.truncated_normal(key_key, -4.0, 4.0, (TOKENS, KVH * HD), jnp.float32)
    values = jax.random.truncated_normal(value_key, -4.0, 4.0, (TOKENS, KVH * HD), jnp.float32)
    return (queries, keys, values)


def draw_queries(key, part):
    queries, keys, values = attention_draw(key)
    return queries.astype(jnp.bfloat16)


def draw_keys_values(key, part):
    queries, keys, values = attention_draw(key)
    return jnp.stack([keys, values]).astype(jnp.bfloat16)


def levels(stream_key, shape, shards, low, largest):
    gain = 1.0
    for dim, parts in shards:
        heights = jax.random.uniform(jax.random.fold_in(jax.random.fold_in(stream_key, 6), dim), (parts,), jnp.float32, low / len(shards), largest / len(shards))
        gain = gain * jnp.repeat(jnp.exp(heights), shape[dim] // parts).reshape((-1,) + (1,) * (len(shape) - 1 - dim))
    return gain


def shared_out(key, own, number, rows, amount, top, bound, slope):
    order = jax.random.permutation(key, amount)
    heavy_load, usual = shares(amount, rows * top, bound, slope, True), shares(amount, rows * top, bound, slope, False)
    places = jnp.arange(amount)

    def named(sizes, turn):
        used = int((sizes > 0).sum())
        fixed = max(1, used // 4)
        passed = fixed + (places - fixed + turn * (used - fixed)) % max(1, amount - fixed)
        return jnp.zeros((amount,), jnp.int32).at[order[jnp.where(places < fixed, places, passed)]].set(jnp.asarray(sizes, jnp.int32))

    sizes = jnp.where(number % 4 == 0, named(heavy_load, number // 4), named(usual, number - number // 4 - 1))
    mixed = jax.random.permutation(jax.random.fold_in(own, 3), amount)
    giver, taker = mixed[0:amount // 2 * 2:2], mixed[1:amount // 2 * 2:2]
    margin = jnp.minimum(sizes[giver] - 1, bound - sizes[taker]) // 2
    margin = jnp.where((giver == order[0]) | (taker == order[0]) | (sizes[taker] == 0), 0, jnp.maximum(margin, 0))
    passed = jax.random.randint(jax.random.fold_in(own, 4), (amount // 2,), 0, 1 << 20) % (margin + 1)
    sizes = sizes.at[giver].add(-passed).at[taker].add(passed)
    members = jnp.searchsorted(jnp.cumsum(sizes), jnp.arange(rows * top), side="right").astype(jnp.int32)
    grid = members.reshape(top, rows).T
    grid = grid[jax.random.permutation(jax.random.fold_in(own, 1), rows)]
    turn = jax.random.randint(jax.random.fold_in(own, 2), (rows, 1), 0, top)
    return jnp.take_along_axis(grid, (jnp.arange(top)[None, :] + turn) % top, axis=1)


def shares(number_of, total, limit, lean, full):
    weights = [(1 << 20) // math.isqrt(standing ** lean) + 1 for standing in range(1, number_of + 1)]
    largest = limit if full else min(limit, max(-(-total // number_of), total * weights[0] // sum(weights)))
    least = 1 if total - largest >= number_of - 1 else 0
    counts, rest = [largest] + [least] * (number_of - 1), total - largest - least * (number_of - 1)
    while rest > 0:
        free = [i for i in range(1, number_of) if counts[i] < largest] or [i for i in range(1, number_of) if counts[i] < limit]
        pool, left = sum([weights[i] for i in free]), rest
        for i in free:
            extra = min(limit - counts[i], max(1, left * weights[i] // pool), rest)
            counts[i] = counts[i] + extra
            rest = rest - extra
    return np.array(counts)


def bell_draw(stream_key, extent, scale, reach, cuts=(), kind=jnp.bfloat16):
    result = jax.random.normal(stream_key, extent, jnp.float32) * scale
    if len(cuts) > 0:
        result = levels(stream_key, extent, cuts, -0.22, 0.18) * result
    return jnp.clip(result, min=-reach, max=reach).astype(kind)


def setup_inputs(seed: int = 0) -> dict:
    splits = jax.random.split(jax.random.key(seed), 11)
    queries = draw_queries(jax.random.fold_in(splits[10], 71), 0)
    keys_values = draw_keys_values(jax.random.fold_in(splits[10], 71), 0)
    residual = bell_draw(splits[2], (TOKENS, D), 1.0, 6.0, ((0, 128),))
    norm_gain = jnp.clip(1.0 + 0.18 * jax.random.normal(splits[3], (D,), jnp.float32), 0.1, 1.9)
    route_logit = jnp.clip(-2.0 + 1.0 * jax.random.uniform(splits[4], (TOKENS,), jnp.float32) ** levels(splits[4], (TOKENS,), ((0, 128),), -0.2, 0.2), -2.0, -1.0)
    expert_ids_keys = jax.random.split(jax.random.fold_in(splits[5], 1), TOKENS // TOK_DEV)
    expert_ids_turns = jax.random.permutation(jax.random.fold_in(splits[5], 3), TOKENS // TOK_DEV)
    expert_ids = jax.vmap(lambda own, number: shared_out(jax.random.fold_in(splits[5], 2), own, number, TOK_DEV, EXPERTS, 1, CAP, 2))(expert_ids_keys, expert_ids_turns).reshape((TOKENS, 1))
    out_weight = bell_draw(splits[6], (H * HD, D), (H * HD) ** -0.5, 0.078125, ((0, 4),))
    gate_weight = bell_draw(splits[7], (EXPERTS, D, FF), (D // 9) ** -0.5, 0.25, ((0, 4), (2, 32)))
    up_weight = bell_draw(splits[8], (EXPERTS, D, FF), (D // 9) ** -0.5, 0.25, ((0, 4), (2, 32)))
    down_weight = bell_draw(splits[9], (EXPERTS, FF, D), (FF // 4) ** -0.5, 0.125, ((0, 4), (1, 32)))
    return dict(queries=queries, keys_values=keys_values, residual=residual, norm_gain=norm_gain, route_logit=route_logit, expert_ids=expert_ids, out_weight=out_weight, gate_weight=gate_weight, up_weight=up_weight, down_weight=down_weight)


def reference(queries, keys_values, residual, norm_gain, route_logit, expert_ids, out_weight, gate_weight, up_weight, down_weight):
    group = H // KVH
    position = jnp.arange(TOKENS, dtype=jnp.int32)
    span_id = position // SPAN
    allowed = (span_id[:, None] == span_id[None, :]) & (position[None, :] <= position[:, None])
    scale = 1.0 / HD ** 0.5

    def one_head(head):
        query = lax.dynamic_slice_in_dim(queries, head * HD, HD, 1)
        kv_head = head // group
        key_rows = lax.dynamic_slice_in_dim(keys_values[0], kv_head * HD, HD, 1)
        value_rows = lax.dynamic_slice_in_dim(keys_values[1], kv_head * HD, HD, 1)
        score = jnp.dot(query, key_rows.T, preferred_element_type=jnp.float32) * scale
        score = jnp.where(allowed, score, -1e+30)
        peak = lax.optimization_barrier(jnp.max(score, axis=1, keepdims=True))
        expo = jnp.where(allowed, jnp.exp(score - peak), 0.0)
        weights = (expo / lax.optimization_barrier(jnp.sum(expo, axis=1, keepdims=True))).astype(jnp.bfloat16)
        return jnp.dot(weights, value_rows, preferred_element_type=jnp.float32)
    heads = lax.map(one_head, jnp.arange(H, dtype=jnp.int32))
    attended = jnp.transpose(heads, (1, 0, 2)).reshape(TOKENS, H * HD).astype(jnp.bfloat16)
    projected = jnp.dot(attended, out_weight, preferred_element_type=jnp.float32)
    mixed = (residual.astype(jnp.float32) + projected).astype(jnp.bfloat16)
    stream = mixed.astype(jnp.float32)
    mean_square = lax.optimization_barrier(jnp.mean(stream * stream, axis=-1, keepdims=True))
    routed_in = (stream * lax.rsqrt(mean_square + 1e-05) * norm_gain * jax.nn.sigmoid(route_logit)[:, None]).astype(jnp.bfloat16)
    blocks = TOKENS // TOK_DEV
    ids = expert_ids[:, 0]
    onehot = (ids.reshape(blocks, TOK_DEV)[..., None] == jnp.arange(EXPERTS, dtype=jnp.int32)).astype(jnp.int32)
    rank = lax.optimization_barrier(jnp.sum((jnp.cumsum(onehot, axis=1) - onehot) * onehot, axis=-1))
    slot = (jnp.arange(blocks, dtype=jnp.int32)[:, None] * CAP + rank).reshape(-1).astype(jnp.int32)
    table = jnp.full((EXPERTS, blocks * CAP), TOKENS, jnp.int32).at[ids, slot].set(jnp.arange(TOKENS, dtype=jnp.int32))
    padded_in = jnp.concatenate([routed_in, jnp.zeros((1, D), jnp.bfloat16)], axis=0)

    def one_expert(expert):
        rows = jnp.take(padded_in, table[expert], axis=0)
        gate = jnp.dot(rows, gate_weight[expert], preferred_element_type=jnp.float32)
        up = jnp.dot(rows, up_weight[expert], preferred_element_type=jnp.float32)
        hidden = (jax.nn.silu(gate) * up).astype(jnp.bfloat16)

        def add_block(block, total):
            hidden_block = lax.dynamic_slice_in_dim(hidden, block * FF_DEV, FF_DEV, 1)
            weight_block = lax.dynamic_slice_in_dim(down_weight[expert], block * FF_DEV, FF_DEV, 0)
            part = jnp.dot(hidden_block, weight_block, preferred_element_type=jnp.float32).astype(jnp.bfloat16)
            part = lax.optimization_barrier(part)
            return total + part.astype(jnp.float32)
        total = lax.fori_loop(0, FF // FF_DEV, add_block, jnp.zeros((rows.shape[0], D), jnp.float32))
        return total.astype(jnp.bfloat16)
    outputs = lax.map(one_expert, jnp.arange(EXPERTS, dtype=jnp.int32))
    routed = jnp.zeros((TOKENS + 1, D), jnp.float32).at[table.reshape(-1)].add(outputs.reshape(-1, D).astype(jnp.float32))[:TOKENS]
    return (stream + routed).astype(jnp.bfloat16)
```

```python
import functools

import jax
import jax.numpy as jnp
from jax import lax
from jax.experimental import pallas as pl
from jax.experimental.pallas import tpu as pltpu
from jax.sharding import Mesh
from jax.sharding import PartitionSpec as P

HD = 128
SEQ = ("z", "x", "core")
BF = jnp.bfloat16
F32 = jnp.float32


def shift(value, axis, by):
    n = lax.axis_size(axis)
    return lax.ppermute(value, axis, [(i, (i + by) % n) for i in range(n)])


def swap(value):
    return lax.ppermute(value, "core", [(0, 1), (1, 0)])


def cat(*parts):
    return jnp.concatenate(parts, axis=0)


def halves(core, value, dim):
    low, high = jnp.split(value, 2, axis=dim)
    first = core == 0
    return jnp.where(first, low, high), jnp.where(first, high, low)


def dot(a, b):
    return jnp.dot(a, b, preferred_element_type=F32)


def attend_kernel(first, last, count, *refs):
    pos_ref, q_ref = refs[:2]
    kv_refs = refs[2 : 2 + count]
    rest = list(refs[2 + count :])
    if not first:
        m_in, l_in, acc_in = rest[:3]
        rest = rest[3:]
    if last:
        (out_ref,) = rest
    else:
        m_out, l_out, acc_out = rest
    rows, width = q_ref.shape
    heads = width // HD
    scale = 1.0 / HD**0.5
    q_pos = pos_ref[0] + lax.broadcasted_iota(jnp.int32, (rows, 1), 0)
    for h in range(heads):
        cols = slice(h * HD, (h + 1) * HD)
        q = q_ref[:, cols]
        if first:
            m = jnp.full((rows, 1), -1e30, F32)
            l = jnp.zeros((rows, 1), F32)
            acc = jnp.zeros((rows, HD), F32)
        else:
            m, l, acc = m_in[h], l_in[h], acc_in[:, cols]
        at = 1
        for kv_ref in kv_refs:
            n = kv_ref.shape[0]
            k_pos = jnp.concatenate(
                [
                    pos_ref[at + i] + lax.broadcasted_iota(jnp.int32, (1, HD), 1)
                    for i in range(n // HD)
                ],
                axis=1,
            )
            at += n // HD
            s = lax.dot_general(
                q, kv_ref[:, :HD], (((1,), (1,)), ((), ())), preferred_element_type=F32
            )
            s = jnp.where(k_pos <= q_pos, s * scale, -1e30)
            top = jnp.maximum(m, jnp.max(s, axis=1, keepdims=True))
            p = jnp.exp(s - top)
            fade = jnp.exp(m - top)
            l = l * fade + jnp.sum(p, axis=1, keepdims=True)
            acc = acc * fade + dot(p.astype(BF), kv_ref[:, HD:])
            m = top
        if last:
            out_ref[:, cols] = (acc / l).astype(BF)
        else:
            m_out[h] = m
            l_out[h] = l
            acc_out[:, cols] = acc


def attend(positions, q, kvs, state, last):
    rows, width = q.shape
    heads = width // HD
    vmem = pl.BlockSpec(memory_space=pltpu.VMEM)
    keys = sum(kv.shape[0] for kv in kvs)
    stat = jax.ShapeDtypeStruct((heads, rows, 1), F32)
    if last:
        out_shape = jax.ShapeDtypeStruct((rows, width), BF)
        out_specs = vmem
    else:
        out_shape = (stat, stat, jax.ShapeDtypeStruct((rows, width), F32))
        out_specs = (vmem,) * 3
    args = [q, *kvs, *(state or ())]
    return pl.pallas_call(
        functools.partial(attend_kernel, state is None, last, len(kvs)),
        out_shape=out_shape,
        in_specs=[pl.BlockSpec(memory_space=pltpu.SMEM)] + [vmem] * len(args),
        out_specs=out_specs,
        cost_estimate=pl.CostEstimate(
            flops=8 * rows * width * keys,
            bytes_accessed=2 * rows * width * 6 + keys * 512,
            transcendentals=rows * heads * keys,
        ),
        compiler_params=pltpu.CompilerParams(vmem_limit_bytes=32 * 2**20),
        name="attend",
    )(positions, *args)


def spread_first(block, axis):
    third = block.shape[0] // 2
    up = shift(block, axis, 1)
    down = shift(block, axis, -1)
    far = (shift(up[:third], axis, 1), shift(down[third:], axis, -1))
    return cat(block, up, down, *far)


def body(
    queries,
    keys_values,
    residual,
    norm_gain,
    route_logit,
    expert_ids,
    out_weight,
    gate_weight,
    up_weight,
    down_weight,
):
    core = lax.axis_index("core")
    zi, xi = lax.axis_index("z"), lax.axis_index("x")
    ey = lax.axis_index("exp")
    experts = lax.axis_size("exp")
    nx = lax.axis_size("x")
    nz = lax.axis_size("z")
    rows = queries.shape[0]
    tokens = residual.shape[0]
    cap = 3 * tokens // 8
    model = residual.shape[1]
    half = model // 2

    q_keep, q_give = halves(core, queries, 1)
    k_keep, k_give = halves(core, keys_values[0], 1)
    v_keep, v_give = halves(core, keys_values[1], 1)
    width = q_keep.shape[1]
    keep = jnp.concatenate([k_keep, v_keep, q_keep], axis=1)
    got = swap(jnp.concatenate([k_give, v_give, q_give], axis=1))
    even = jnp.where(core == 0, keep, got)
    odd = jnp.where(core == 0, got, keep)
    q_rows = cat(even[:, 2 * HD :], odd[:, 2 * HD :])

    chip = zi * nx + xi

    def place(dz, dx, which):
        z, x = (zi + dz) % nz, (xi + dx) % nx
        return (z * nx + x) * 2 * rows + which * rows

    OFF = (0, -1, 1, 2)
    base = chip * 2 * rows

    def places(second):
        out = []
        for g in second:
            out += [place(g, d, 0) for d in OFF]
            out += [place(d, g, 1) for d in OFF]
        return jnp.stack([base] + out).astype(jnp.int32)

    def kv_first(block, axis):
        return cat(
            block, shift(block, axis, 1), shift(block, axis, -1), shift(block, axis, 2)
        )

    kv_a = kv_first(even[:, : 2 * HD], "x")
    kv_b = kv_first(odd[:, : 2 * HD], "z")
    state = attend(places((0,)), q_rows, [kv_a, kv_b], None, False)
    a_up, a_down = shift(kv_a, "z", 1), shift(kv_a, "z", -1)
    b_up, b_down = shift(kv_b, "x", 1), shift(kv_b, "x", -1)
    mid = kv_a.shape[0] // 2
    a_far = cat(shift(a_up[:mid], "z", 1), shift(a_down[mid:], "z", -1))
    b_far = cat(shift(b_up[:mid], "x", 1), shift(b_down[mid:], "x", -1))
    state = attend(places((-1, 1)), q_rows, [a_up, b_up, a_down, b_down], state, False)
    mine = attend(places((2,)), q_rows, [a_far, b_far], state, True)

    ids = expert_ids[:, 0]
    onehot = (ids[:, None] == jnp.arange(experts, dtype=jnp.int32)[None, :]).astype(F32)
    before = (
        jnp.arange(tokens)[:, None] > jnp.arange(tokens)[None, :]
    ).astype(F32)
    rank = jnp.sum(jnp.dot(before, onehot) * onehot, axis=1)
    info = jnp.stack([ids.astype(F32), rank, route_logit])
    by_offset = [info] + [shift(info, "exp", k) for k in (1, 2, 3)]
    turned = jnp.stack(by_offset[::-1] * 2)
    info_all = lax.dynamic_slice_in_dim(turned, (3 - ey) % experts, experts, 0)
    info_other = swap(info_all)
    info_chip = jnp.stack(
        [
            jnp.where(core == 0, info_all, info_other),
            jnp.where(core == 0, info_other, info_all),
        ]
    )
    chip_ids = info_chip[:, :, 0].astype(jnp.int32)
    chip_rank = info_chip[:, :, 1].astype(jnp.int32)
    chip_logit = info_chip[:, :, 2]
    home = jnp.arange(experts, dtype=jnp.int32)[None, :, None]
    which = jnp.arange(2, dtype=jnp.int32)[:, None, None]
    seat = (
        which * experts * cap + ((home - chip_ids) % experts) * cap + chip_rank
    )
    seats = 2 * experts * cap
    turn = (chip_ids - ey) % experts
    seat_flat = seat.reshape(-1)
    turn_flat = turn.reshape(-1)
    seat_row = jnp.arange(seats, dtype=jnp.int32)[:, None]

    def placing(k):
        return (turn_flat[None, :] == k) & (seat_row == seat_flat[None, :])

    their = swap(mine)
    att = jnp.concatenate(
        [jnp.where(core == 0, mine, their), jnp.where(core == 0, their, mine)], axis=1
    )
    w_half, _ = halves(core, out_weight, 1)
    r_keep, r_give = halves(core, residual, 1)
    r_got = swap(r_give)
    res = cat(jnp.where(core == 0, r_keep, r_got), jnp.where(core == 0, r_got, r_keep))
    own_ids = lax.dynamic_slice_in_dim(chip_ids, ey, 1, 1).reshape(-1)
    own_seat = lax.dynamic_slice_in_dim(seat, ey, 1, 1).reshape(-1)
    own_turn = (own_ids - ey) % experts

    def part(k):
        picked = dot(placing(k).astype(BF), att).astype(BF)
        own = ((own_turn[None, :] == k) & (seat_row == own_seat[None, :])).astype(BF)
        return (dot(picked, w_half) + dot(own, res)).astype(BF)

    far_part = shift(part(2), "exp", 2)
    up_part = shift(part(1), "exp", 1)
    down_part = shift(part(3), "exp", 3)
    mixed = (
        part(0).astype(F32)
        + up_part.astype(F32)
        + down_part.astype(F32)
        + far_part.astype(F32)
    ).astype(BF)
    stream = mixed.astype(F32)
    squares = jnp.sum(stream * stream, axis=-1, keepdims=True)
    mean_square = (squares + swap(squares)) / model
    gain_half, _ = halves(core, norm_gain, 0)
    here = placing(0).astype(F32)
    logit = jnp.sum(here * chip_logit.reshape(-1)[None, :], axis=1, keepdims=True)
    routed_in = (
        stream * lax.rsqrt(mean_square + 1e-05) * gain_half[None, :] * jax.nn.sigmoid(logit)
    ).astype(BF)

    g_keep, g_give = halves(core, gate_weight[0], 0)
    u_keep, u_give = halves(core, up_weight[0], 0)
    d_keep, d_give = halves(core, down_weight[0], 1)
    w_own = jnp.concatenate([g_keep, u_keep], axis=1)
    w_other = swap(jnp.concatenate([g_give, u_give], axis=1))
    d_both = cat(d_keep, swap(d_give))
    hid = gate_weight.shape[2]

    def expert(x):
        sent = swap(dot(x, w_other).astype(BF))
        gu = dot(x, w_own) + sent.astype(F32)
        hidden = (jax.nn.silu(gu[:, :hid]) * gu[:, hid:]).astype(BF)
        both = jnp.concatenate([hidden, swap(hidden)], axis=1)
        return dot(both, d_both).astype(BF)

    n = routed_in.shape[0] // 2
    a0 = spread_first(routed_in[:n], "x")
    b0 = spread_first(routed_in[n:], "z")
    au, ad = shift(a0, "z", 1), shift(a0, "z", -1)
    bu, bd = shift(b0, "x", 1), shift(b0, "x", -1)
    m = a0.shape[0] // 2
    af = cat(shift(au[:m], "z", 1), shift(ad[m:], "z", -1))
    bf = cat(shift(bu[:m], "x", 1), shift(bd[m:], "x", -1))
    t0 = expert(cat(a0, b0))
    t1 = expert(cat(au, bu, ad, bd))
    t2 = expert(cat(af, bf))

    def plus(a, b):
        return (a.astype(F32) + b.astype(F32)).astype(BF)

    def sum_first(t, axis):
        k = n // 2
        far_low = shift(t[:, 3, :k], axis, -1)
        far_high = shift(t[:, 3, k:], axis, 1)
        to_down = jnp.concatenate([plus(t[:, 1, :k], far_low), t[:, 1, k:]], axis=1)
        to_up = jnp.concatenate([t[:, 2, :k], plus(t[:, 2, k:], far_high)], axis=1)
        from_up = shift(to_down, axis, -1)
        from_down = shift(to_up, axis, 1)
        return t[:, 0].astype(F32) + from_up.astype(F32) + from_down.astype(F32)

    def groups(t):
        return t.reshape(-1, 2, 4, n, half)

    def reduce_group(t):
        t = groups(t)
        return (
            sum_first(t[:, 0], "x").astype(BF),
            sum_first(t[:, 1], "z").astype(BF),
        )

    g0, g1, g2 = reduce_group(t0), reduce_group(t1), reduce_group(t2)
    done = []
    for i, axis in enumerate(("z", "x")):
        line = cat(g0[i], g1[i], g2[i])[None]
        done.append(sum_first(line, axis)[0])
    final = (stream + cat(*done)).astype(BF)

    f_keep, f_give = jnp.where(core == 0, final[:n], final[n:]), jnp.where(
        core == 0, final[n:], final[:n]
    )
    f_got = swap(f_give)
    full = jnp.concatenate(
        [jnp.where(core == 0, f_keep, f_got), jnp.where(core == 0, f_got, f_keep)], axis=1
    )
    blocks = [full[r * cap : (r + 1) * cap] for r in range(experts)]
    back = cat(blocks[0], *[shift(blocks[r], "exp", r) for r in (1, 2, 3)])
    index = ((ey - ids) % experts) * cap + rank.astype(jnp.int32)
    picking = (
        index[:, None] == jnp.arange(experts * cap, dtype=jnp.int32)[None, :]
    ).astype(BF)
    return dot(picking, back).astype(BF)


def solution(mesh):
    devices = mesh.devices
    seq, exp = devices.shape
    grid = Mesh(devices.reshape(4, seq // 8, 2, exp), SEQ + ("exp",))
    in_specs = (
        P(SEQ, "exp"),
        P(None, SEQ, "exp"),
        P(SEQ + ("exp",), None),
        P(),
        P(SEQ + ("exp",)),
        P(SEQ + ("exp",), None),
        P("exp", None),
        P("exp", None, SEQ),
        P("exp", None, SEQ),
        P("exp", SEQ, None),
    )
    out_specs = P(SEQ + ("exp",), None)
    return jax.shard_map(body, mesh=grid, in_specs=in_specs, out_specs=out_specs, check_vma=False)
```

```python
import functools

import jax
import jax.numpy as jnp
from jax import lax
from jax.experimental import pallas as pl
from jax.experimental.pallas import tpu as pltpu
from jax.sharding import Mesh
from jax.sharding import PartitionSpec as P


HD = 128
LOG2E = 1.4426950408889634
SEQ = ("z", "x", "core")
BF = jnp.bfloat16
F32 = jnp.float32


def shift(value, axis, by):
    n = lax.axis_size(axis)
    return lax.ppermute(value, axis, [(i, (i + by) % n) for i in range(n)])


def swap(value):
    return lax.ppermute(value, "core", [(0, 1), (1, 0)])


def cat(*parts):
    return jnp.concatenate(parts, axis=0)


def halves(core, value, dim):
    low, high = jnp.split(value, 2, axis=dim)
    first = core == 0
    return jnp.where(first, low, high), jnp.where(first, high, low)


def dot(a, b):
    return jnp.dot(a, b, preferred_element_type=F32)


def attend_kernel(first, last, count, *refs):
    pos_ref, q_ref = refs[:2]
    kv_refs = refs[2 : 2 + count]
    rest = list(refs[2 + count :])
    if not first:
        m_in, l_in, acc_in = rest[:3]
        rest = rest[3:]
    if last:
        (out_ref,) = rest
    else:
        m_out, l_out, acc_out = rest
    rows, width = q_ref.shape
    heads = width // HD
    scale = LOG2E / HD**0.5
    base = pos_ref[0]
    q_pos = base + lax.broadcasted_iota(jnp.int32, (rows, 1), 0)

    def head(h, carry):
        cols = pl.ds(pl.multiple_of(h * HD, HD), HD)
        q = q_ref[:, cols]
        if first:
            m = jnp.full((rows, 1), -1e30, F32)
            l = jnp.zeros((rows, 1), F32)
            acc = jnp.zeros((rows, HD), F32)
        else:
            m, l, acc = m_in[h], l_in[h], acc_in[:, cols]
        at = 1
        lane = lax.broadcasted_iota(jnp.int32, (1, HD), 1)
        scores = []
        for kv_ref in kv_refs:
            n = kv_ref.shape[0]
            starts = [pos_ref[at + i] for i in range(n // HD)]
            at += n // HD
            s = lax.dot_general(
                q, kv_ref[:, :HD], (((1,), (1,)), ((), ())), preferred_element_type=F32
            )
            if first:
                k_pos = jnp.concatenate([p + lane for p in starts], axis=1)
                s = jnp.where(k_pos <= q_pos, s * scale, -1e30)
            else:
                bias = jnp.concatenate(
                    [jnp.where(p + 0 * lane < base, 0.0, -1e30) for p in starts], axis=1
                )
                s = s * scale + bias
            scores.append(s)
        tops = [jnp.max(s, axis=1, keepdims=True) for s in scores]
        top = functools.reduce(jnp.maximum, tops, m)
        fade = jnp.exp2(m - top)
        l = l * fade
        acc = acc * fade
        for s, kv_ref in zip(scores, kv_refs):
            p = jnp.exp2(s - top)
            l = l + jnp.sum(p, axis=1, keepdims=True)
            acc = acc + dot(p.astype(BF), kv_ref[:, HD:])
        m = top
        if last:
            out_ref[:, cols] = (acc / l).astype(BF)
        else:
            m_out[h] = m
            l_out[h] = l
            acc_out[:, cols] = acc
        return carry

    lax.fori_loop(0, heads, head, 0)


def attend(positions, q, kvs, state, last):
    rows, width = q.shape
    heads = width // HD
    vmem = pl.BlockSpec(memory_space=pltpu.VMEM)
    keys = sum(kv.shape[0] for kv in kvs)
    stat = jax.ShapeDtypeStruct((heads, rows, 1), F32)
    if last:
        out_shape = jax.ShapeDtypeStruct((rows, width), BF)
        out_specs = vmem
    else:
        out_shape = (stat, stat, jax.ShapeDtypeStruct((rows, width), F32))
        out_specs = (vmem,) * 3
    args = [q, *kvs, *(state or ())]
    return pl.pallas_call(
        functools.partial(attend_kernel, state is None, last, len(kvs)),
        out_shape=out_shape,
        in_specs=[pl.BlockSpec(memory_space=pltpu.SMEM)] + [vmem] * len(args),
        out_specs=out_specs,
        cost_estimate=pl.CostEstimate(
            flops=8 * rows * width * keys,
            bytes_accessed=2 * rows * width * 6 + keys * 512,
            transcendentals=rows * heads * keys,
        ),
        compiler_params=pltpu.CompilerParams(vmem_limit_bytes=32 * 2**20),
        name="attend",
    )(positions, *args)


def along(block, axis):
    return cat(
        block, shift(block, axis, 1), shift(block, axis, -1), shift(block, axis, 2)
    )


def my_half(core, value, dim, other=False):
    size = value.shape[dim] // 2
    at = (1 - core if other else core) * size
    return lax.dynamic_slice_in_dim(value, at, size, dim)


def layer(
    queries,
    keys_values,
    residual,
    norm_gain,
    route_logit,
    expert_ids,
    out_weight,
    gate_weight,
    up_weight,
    down_weight,
):
    core = lax.axis_index("core")
    zi, xi = lax.axis_index("z"), lax.axis_index("x")
    ey = lax.axis_index("exp")
    experts = lax.axis_size("exp")
    nx = lax.axis_size("x")
    nz = lax.axis_size("z")
    rows = queries.shape[0]
    tokens = residual.shape[0]
    cap = 3 * tokens // 8
    model = residual.shape[1]
    half = model // 2

    def kv_half(other):
        pair = [my_half(core, keys_values[i], 1, other) for i in (0, 1)]
        return jnp.concatenate(pair, axis=1)

    kv_keep, kv_got = kv_half(False), swap(kv_half(True))
    kv_chip = cat(
        jnp.where(core == 0, kv_keep, kv_got), jnp.where(core == 0, kv_got, kv_keep)
    )
    q_keep, q_got = my_half(core, queries, 1), swap(my_half(core, queries, 1, True))
    q_rows = cat(jnp.where(core == 0, q_keep, q_got), jnp.where(core == 0, q_got, q_keep))

    chip = zi * nx + xi

    def place(dz, dx, which):
        z, x = (zi + dz) % nz, (xi + dx) % nx
        return (z * nx + x) * 2 * rows + which * rows

    OFF = (0, -1, 1, 2)
    base = chip * 2 * rows

    def places(second):
        out = []
        for g in second:
            out += [place(g, d, which) for d in OFF for which in (0, 1)]
        return jnp.stack([base] + out).astype(jnp.int32)

    kv_row = along(kv_chip, "x")
    kv_row, residual, route_logit, expert_ids = lax.optimization_barrier(
        (kv_row, residual, route_logit, expert_ids)
    )
    kv_up, kv_down, kv_far = (
        shift(kv_row, "z", k) for k in (1, -1, 2)
    )
    ids = expert_ids[:, 0]
    onehot = (ids[:, None] == jnp.arange(experts, dtype=jnp.int32)[None, :]).astype(F32)
    before = (
        jnp.arange(tokens)[:, None] > jnp.arange(tokens)[None, :]
    ).astype(F32)
    rank = jnp.sum(jnp.dot(before, onehot) * onehot, axis=1)
    info = jnp.stack([ids.astype(F32), rank, route_logit])
    by_offset = [info] + [shift(info, "exp", k) for k in (1, 2, 3)]
    turned = jnp.stack(by_offset[::-1] * 2)
    info_all = lax.dynamic_slice_in_dim(turned, (3 - ey) % experts, experts, 0)
    info_other = swap(info_all)
    info_chip = jnp.stack(
        [
            jnp.where(core == 0, info_all, info_other),
            jnp.where(core == 0, info_other, info_all),
        ]
    )
    chip_ids = info_chip[:, :, 0].astype(jnp.int32)
    chip_rank = info_chip[:, :, 1].astype(jnp.int32)
    chip_logit = info_chip[:, :, 2]
    home = jnp.arange(experts, dtype=jnp.int32)[None, :, None]
    which = jnp.arange(2, dtype=jnp.int32)[:, None, None]
    seat = (
        which * experts * cap + ((home - chip_ids) % experts) * cap + chip_rank
    )
    seats = 2 * experts * cap
    turn = (chip_ids - ey) % experts
    seat_flat = seat.reshape(-1)
    turn_flat = turn.reshape(-1)
    seat_row = jnp.arange(seats, dtype=jnp.int32)[:, None]

    def placing(k):
        return (turn_flat[None, :] == k) & (seat_row == seat_flat[None, :])

    r_keep, r_give = my_half(core, residual, 1), my_half(core, residual, 1, True)
    r_got = swap(r_give)
    res = cat(jnp.where(core == 0, r_keep, r_got), jnp.where(core == 0, r_got, r_keep))
    own_ids = lax.dynamic_slice_in_dim(chip_ids, ey, 1, 1).reshape(-1)
    own_seat = lax.dynamic_slice_in_dim(seat, ey, 1, 1).reshape(-1)
    own_turn = (own_ids - ey) % experts
    all_rows = jnp.arange(experts * seats, dtype=jnp.int32)[:, None]
    placed = (all_rows == (turn_flat * seats + seat_flat)[None, :]).astype(BF)
    own = (all_rows == (own_turn * seats + own_seat)[None, :]).astype(BF)
    kept = dot(own, res).astype(BF)
    q_rows, placed, kept = lax.optimization_barrier((q_rows, placed, kept))
    state = attend(places((0,)), q_rows, [kv_row], None, False)
    state = attend(places((-1, 1)), q_rows, [kv_up, kv_down], state, False)
    mine = attend(places((2,)), q_rows, [kv_far], state, True)
    their = swap(mine)
    att = jnp.concatenate(
        [jnp.where(core == 0, mine, their), jnp.where(core == 0, their, mine)], axis=1
    )
    picked = lax.optimization_barrier(dot(placed, att).astype(BF))
    parts = (dot(picked, my_half(core, out_weight, 1)) + kept.astype(F32)).astype(BF)
    parts, gate_weight, up_weight, down_weight = lax.optimization_barrier(
        (parts, gate_weight, up_weight, down_weight)
    )
    parts = parts.reshape(experts, seats, half)
    far_part = shift(parts[2], "exp", 2)
    up_part = shift(parts[1], "exp", 1)
    down_part = shift(parts[3], "exp", 3)
    mixed = (
        parts[0].astype(F32)
        + up_part.astype(F32)
        + down_part.astype(F32)
        + far_part.astype(F32)
    ).astype(BF)
    stream = mixed.astype(F32)
    squares = jnp.sum(stream * stream, axis=-1, keepdims=True)
    mean_square = (squares + swap(squares)) / model
    gain_half, _ = halves(core, norm_gain, 0)
    here = placing(0).astype(F32)
    logit = jnp.sum(here * chip_logit.reshape(-1)[None, :], axis=1, keepdims=True)
    routed_in = (
        stream * lax.rsqrt(mean_square + 1e-05) * gain_half[None, :] * jax.nn.sigmoid(logit)
    ).astype(BF)

    w_own = jnp.concatenate(
        [my_half(core, gate_weight[0], 0), my_half(core, up_weight[0], 0)], axis=1
    )
    w_other = swap(
        jnp.concatenate(
            [my_half(core, gate_weight[0], 0, True), my_half(core, up_weight[0], 0, True)],
            axis=1,
        )
    )
    d_both = cat(
        my_half(core, down_weight[0], 1), swap(my_half(core, down_weight[0], 1, True))
    )
    hid = gate_weight.shape[2]

    def expert(x):
        sent = dot(x, w_other).astype(BF)
        sent = swap(sent)
        gu = dot(x, w_own) + sent.astype(F32)
        hidden = (jax.nn.silu(gu[:, :hid]) * gu[:, hid:]).astype(BF)
        both = jnp.concatenate([hidden, swap(hidden)], axis=1)
        return dot(both, d_both).astype(BF)

    n = routed_in.shape[0] // 2
    a0, b0 = lax.optimization_barrier(
        (along(routed_in[:n], "x"), along(routed_in[n:], "z"))
    )
    ring = {}
    for key, rows0, axis in (("a", a0, "z"), ("b", b0, "x")):
        low, high = rows0[: 2 * n], rows0[2 * n :]
        up_low = shift(low, axis, 1)
        down_high = shift(high, axis, -1)
        up_high = shift(high, axis, 1)
        down_low = shift(low, axis, -1)
        far_low = shift(up_low, axis, 1)
        far_high = shift(down_high, axis, -1)
        ring[key] = ((up_low, down_high), (up_high, down_low), (far_low, far_high))
    (a1, a2, a3), (b1, b2, b3) = ring["a"], ring["b"]
    t0 = expert(cat(a0, b0))
    t1 = expert(cat(*a1, *b1))
    more, t1 = lax.optimization_barrier((cat(*a2, *b2), t1))
    t2 = expert(more)
    last_rows, t2 = lax.optimization_barrier((cat(*a3, *b3), t2))
    t3 = expert(last_rows)
    t0, t1, t2, t3 = (t.reshape(2, 4, n, half) for t in (t0, t1, t2, t3))

    def plus(a, b):
        return (a.astype(F32) + b.astype(F32)).astype(BF)

    def sum_first(sets):
        k = n // 2
        axes = ("x", "z")
        ends = [
            (cat(*[g[3][:k] for g in groups]), cat(*[g[3][k:] for g in groups]))
            for groups in sets
        ]
        ends = lax.optimization_barrier(ends)
        got = [
            (shift(low, axis, -1), shift(high, axis, 1))
            for axis, (low, high) in zip(axes, ends)
        ]
        out = []
        for axis, groups, (low, high) in zip(axes, sets, got):
            to_down, to_up = [], []
            for i, g in enumerate(groups):
                to_down += [plus(g[1][:k], low[i * k : (i + 1) * k]), g[1][k:]]
                to_up += [g[2][:k], plus(g[2][k:], high[i * k : (i + 1) * k])]
            from_up = shift(cat(*to_down), axis, -1)
            from_down = shift(cat(*to_up), axis, 1)
            own = cat(*[g[0] for g in groups]).astype(F32)
            total = (own + from_up.astype(F32) + from_down.astype(F32)).astype(BF)
            out.append(total.reshape(len(groups), n, half))
        return out

    def sum_direct(t, axis):
        far = shift(t[3], axis, 2)
        return (
            t[0].astype(F32)
            + shift(t[1], axis, -1).astype(F32)
            + shift(t[2], axis, 1).astype(F32)
            + far.astype(F32)
        )

    sets = []
    for i in range(2):
        zero = [t0[i][o] for o in range(4)]
        minus = [t1[i][0], t1[i][1], t2[i][0], t2[i][1]]
        plus_one = [t2[i][2], t2[i][3], t1[i][2], t1[i][3]]
        sets.append([zero, minus, plus_one])
    g1 = sum_first(sets)
    g2 = [sum_direct(t3[i], axis).astype(BF) for i, axis in enumerate(("x", "z"))]
    done = []
    for i, axis in enumerate(("z", "x")):
        done.append(sum_direct((g1[i][0], g1[i][1], g1[i][2], g2[i]), axis))
    final = (stream + cat(*done)).astype(BF)

    f_keep, f_give = jnp.where(core == 0, final[:n], final[n:]), jnp.where(
        core == 0, final[n:], final[:n]
    )
    f_got = swap(f_give)
    full = jnp.concatenate(
        [jnp.where(core == 0, f_keep, f_got), jnp.where(core == 0, f_got, f_keep)], axis=1
    )
    blocks = [full[r * cap : (r + 1) * cap] for r in range(experts)]
    back = cat(blocks[0], *[shift(blocks[r], "exp", r) for r in (1, 2, 3)])
    index = ((ey - ids) % experts) * cap + rank.astype(jnp.int32)
    picking = (
        index[:, None] == jnp.arange(experts * cap, dtype=jnp.int32)[None, :]
    ).astype(BF)
    return dot(picking, back).astype(BF)


def solution(mesh):
    devices = mesh.devices
    seq, exp = devices.shape
    grid = Mesh(devices.reshape(4, seq // 8, 2, exp), SEQ + ("exp",))
    in_specs = (
        P(SEQ, "exp"),
        P(None, SEQ, "exp"),
        P(SEQ + ("exp",), None),
        P(),
        P(SEQ + ("exp",)),
        P(SEQ + ("exp",), None),
        P("exp", None),
        P("exp", None, SEQ),
        P("exp", None, SEQ),
        P("exp", SEQ, None),
    )
    out_specs = P(SEQ + ("exp",), None)
    return jax.shard_map(
        layer, mesh=grid, in_specs=in_specs, out_specs=out_specs, check_vma=False
    )
```

```python
import functools

import jax
import jax.numpy as jnp
from jax import lax
from jax.experimental import pallas as pl
from jax.experimental.pallas import tpu as pltpu
from jax.sharding import Mesh
from jax.sharding import PartitionSpec as P


HD = 128
LOG2E = 1.4426950408889634
SEQ = ("z", "x", "core")
BF = jnp.bfloat16
F32 = jnp.float32


def shift(value, axis, by):
    n = lax.axis_size(axis)
    return lax.ppermute(value, axis, [(i, (i + by) % n) for i in range(n)])


def swap(value):
    return lax.ppermute(value, "core", [(0, 1), (1, 0)])


def cat(*parts):
    return jnp.concatenate(parts, axis=0)


def halves(core, value, dim):
    low, high = jnp.split(value, 2, axis=dim)
    first = core == 0
    return jnp.where(first, low, high), jnp.where(first, high, low)


def dot(a, b):
    return jnp.dot(a, b, preferred_element_type=F32)


def attend_kernel(first, last, count, *refs):
    pos_ref, q_ref = refs[:2]
    kv_refs = refs[2 : 2 + count]
    rest = list(refs[2 + count :])
    if not first:
        m_in, l_in, acc_in = rest[:3]
        rest = rest[3:]
    if last:
        (out_ref,) = rest
    else:
        m_out, l_out, acc_out = rest
    rows, width = q_ref.shape
    heads = width // HD
    scale = LOG2E / HD**0.5
    base = pos_ref[0]
    q_pos = base + lax.broadcasted_iota(jnp.int32, (rows, 1), 0)

    def head(h, carry):
        cols = pl.ds(pl.multiple_of(h * HD, HD), HD)
        q = q_ref[:, cols]
        if first:
            m = jnp.full((rows, 1), -1e30, F32)
            l = jnp.zeros((rows, 1), F32)
            acc = jnp.zeros((rows, HD), F32)
        else:
            m, l, acc = m_in[h], l_in[h], acc_in[:, cols]
        at = 1
        lane = lax.broadcasted_iota(jnp.int32, (1, HD), 1)
        scores = []
        for kv_ref in kv_refs:
            n = kv_ref.shape[0]
            starts = [pos_ref[at + i] for i in range(n // HD)]
            at += n // HD
            s = lax.dot_general(
                q, kv_ref[:, :HD], (((1,), (1,)), ((), ())), preferred_element_type=F32
            )
            if first:
                k_pos = jnp.concatenate([p + lane for p in starts], axis=1)
                s = jnp.where(k_pos <= q_pos, s * scale, -1e30)
            else:
                bias = jnp.concatenate(
                    [jnp.where(p + 0 * lane < base, 0.0, -1e30) for p in starts], axis=1
                )
                s = s * scale + bias
            scores.append(s)
        tops = [jnp.max(s, axis=1, keepdims=True) for s in scores]
        top = functools.reduce(jnp.maximum, tops, m)
        fade = jnp.exp2(m - top)
        l = l * fade
        acc = acc * fade
        for s, kv_ref in zip(scores, kv_refs):
            p = jnp.exp2(s - top)
            l = l + jnp.sum(p, axis=1, keepdims=True)
            acc = acc + dot(p.astype(BF), kv_ref[:, HD:])
        m = top
        if last:
            out_ref[:, cols] = (acc / l).astype(BF)
        else:
            m_out[h] = m
            l_out[h] = l
            acc_out[:, cols] = acc
        return carry

    lax.fori_loop(0, heads, head, 0)


def attend(positions, q, kvs, state, last):
    rows, width = q.shape
    heads = width // HD
    vmem = pl.BlockSpec(memory_space=pltpu.VMEM)
    keys = sum(kv.shape[0] for kv in kvs)
    stat = jax.ShapeDtypeStruct((heads, rows, 1), F32)
    if last:
        out_shape = jax.ShapeDtypeStruct((rows, width), BF)
        out_specs = vmem
    else:
        out_shape = (stat, stat, jax.ShapeDtypeStruct((rows, width), F32))
        out_specs = (vmem,) * 3
    args = [q, *kvs, *(state or ())]
    return pl.pallas_call(
        functools.partial(attend_kernel, state is None, last, len(kvs)),
        out_shape=out_shape,
        in_specs=[pl.BlockSpec(memory_space=pltpu.SMEM)] + [vmem] * len(args),
        out_specs=out_specs,
        cost_estimate=pl.CostEstimate(
            flops=8 * rows * width * keys,
            bytes_accessed=2 * rows * width * 6 + keys * 512,
            transcendentals=rows * heads * keys,
        ),
        compiler_params=pltpu.CompilerParams(vmem_limit_bytes=32 * 2**20),
        name="attend",
    )(positions, *args)


def along(block, axis):
    return cat(
        block, shift(block, axis, 1), shift(block, axis, -1), shift(block, axis, 2)
    )


def my_half(core, value, dim, other=False):
    size = value.shape[dim] // 2
    at = (1 - core if other else core) * size
    return lax.dynamic_slice_in_dim(value, at, size, dim)


def layer(
    queries,
    keys_values,
    residual,
    norm_gain,
    route_logit,
    expert_ids,
    out_weight,
    gate_weight,
    up_weight,
    down_weight,
):
    core = lax.axis_index("core")
    zi, xi = lax.axis_index("z"), lax.axis_index("x")
    ey = lax.axis_index("exp")
    experts = lax.axis_size("exp")
    nx = lax.axis_size("x")
    nz = lax.axis_size("z")
    rows = queries.shape[0]
    tokens = residual.shape[0]
    cap = 3 * tokens // 8
    model = residual.shape[1]
    half = model // 2

    def kv_half(other):
        pair = [my_half(core, keys_values[i], 1, other) for i in (0, 1)]
        return jnp.concatenate(pair, axis=1)

    kv_keep, kv_got = kv_half(False), swap(kv_half(True))
    kv_chip = cat(
        jnp.where(core == 0, kv_keep, kv_got), jnp.where(core == 0, kv_got, kv_keep)
    )
    q_keep, q_got = my_half(core, queries, 1), swap(my_half(core, queries, 1, True))
    q_rows = cat(jnp.where(core == 0, q_keep, q_got), jnp.where(core == 0, q_got, q_keep))

    chip = zi * nx + xi

    def place(dz, dx, which):
        z, x = (zi + dz) % nz, (xi + dx) % nx
        return (z * nx + x) * 2 * rows + which * rows

    OFF = (0, -1, 1, 2)
    base = chip * 2 * rows

    def places(second):
        out = []
        for g in second:
            out += [place(g, d, which) for d in OFF for which in (0, 1)]
        return jnp.stack([base] + out).astype(jnp.int32)

    kv_row = along(kv_chip, "x")
    kv_row, residual, route_logit, expert_ids = lax.optimization_barrier(
        (kv_row, residual, route_logit, expert_ids)
    )
    kv_up, kv_down, kv_far = (
        shift(kv_row, "z", k) for k in (1, -1, 2)
    )
    ids = expert_ids[:, 0]
    onehot = (ids[:, None] == jnp.arange(experts, dtype=jnp.int32)[None, :]).astype(F32)
    before = (
        jnp.arange(tokens)[:, None] > jnp.arange(tokens)[None, :]
    ).astype(F32)
    rank = jnp.sum(jnp.dot(before, onehot) * onehot, axis=1)
    info = jnp.stack([ids.astype(F32), rank, route_logit])
    by_offset = [info] + [shift(info, "exp", k) for k in (1, 2, 3)]
    turned = jnp.stack(by_offset[::-1] * 2)
    info_all = lax.dynamic_slice_in_dim(turned, (3 - ey) % experts, experts, 0)
    info_other = swap(info_all)
    info_chip = jnp.stack(
        [
            jnp.where(core == 0, info_all, info_other),
            jnp.where(core == 0, info_other, info_all),
        ]
    )
    chip_ids = info_chip[:, :, 0].astype(jnp.int32)
    chip_rank = info_chip[:, :, 1].astype(jnp.int32)
    chip_logit = info_chip[:, :, 2]
    home = jnp.arange(experts, dtype=jnp.int32)[None, :, None]
    which = jnp.arange(2, dtype=jnp.int32)[:, None, None]
    seat = (
        which * experts * cap + ((home - chip_ids) % experts) * cap + chip_rank
    )
    seats = 2 * experts * cap
    turn = (chip_ids - ey) % experts
    seat_flat = seat.reshape(-1)
    turn_flat = turn.reshape(-1)
    seat_row = jnp.arange(seats, dtype=jnp.int32)[:, None]

    def placing(k):
        return (turn_flat[None, :] == k) & (seat_row == seat_flat[None, :])

    r_keep, r_give = my_half(core, residual, 1), my_half(core, residual, 1, True)
    r_got = swap(r_give)
    res = cat(jnp.where(core == 0, r_keep, r_got), jnp.where(core == 0, r_got, r_keep))
    own_ids = lax.dynamic_slice_in_dim(chip_ids, ey, 1, 1).reshape(-1)
    own_seat = lax.dynamic_slice_in_dim(seat, ey, 1, 1).reshape(-1)
    own_turn = (own_ids - ey) % experts
    all_rows = jnp.arange(experts * seats, dtype=jnp.int32)[:, None]
    placed = (all_rows == (turn_flat * seats + seat_flat)[None, :]).astype(BF)
    own = (all_rows == (own_turn * seats + own_seat)[None, :]).astype(BF)
    kept = dot(own, res).astype(BF)
    q_rows, placed, kept = lax.optimization_barrier((q_rows, placed, kept))
    state = attend(places((0,)), q_rows, [kv_row], None, False)
    state = attend(places((-1, 1)), q_rows, [kv_up, kv_down], state, False)
    mine = attend(places((2,)), q_rows, [kv_far], state, True)
    their = swap(mine)
    att = jnp.concatenate(
        [jnp.where(core == 0, mine, their), jnp.where(core == 0, their, mine)], axis=1
    )
    picked = lax.optimization_barrier(dot(placed, att).astype(BF))
    parts = (dot(picked, my_half(core, out_weight, 1)) + kept.astype(F32)).astype(BF)
    parts, gate_weight, up_weight, down_weight = lax.optimization_barrier(
        (parts, gate_weight, up_weight, down_weight)
    )
    parts = parts.reshape(experts, seats, half)
    far_part = shift(parts[2], "exp", 2)
    up_part = shift(parts[1], "exp", 1)
    down_part = shift(parts[3], "exp", 3)
    mixed = (
        parts[0].astype(F32)
        + up_part.astype(F32)
        + down_part.astype(F32)
        + far_part.astype(F32)
    ).astype(BF)
    stream = mixed.astype(F32)
    squares = jnp.sum(stream * stream, axis=-1, keepdims=True)
    mean_square = (squares + swap(squares)) / model
    gain_half, _ = halves(core, norm_gain, 0)
    here = placing(0).astype(F32)
    logit = jnp.sum(here * chip_logit.reshape(-1)[None, :], axis=1, keepdims=True)
    routed_in = (
        stream * lax.rsqrt(mean_square + 1e-05) * gain_half[None, :] * jax.nn.sigmoid(logit)
    ).astype(BF)

    w_own = jnp.concatenate(
        [my_half(core, gate_weight[0], 0), my_half(core, up_weight[0], 0)], axis=1
    )
    w_other = swap(
        jnp.concatenate(
            [my_half(core, gate_weight[0], 0, True), my_half(core, up_weight[0], 0, True)],
            axis=1,
        )
    )
    d_both = cat(
        my_half(core, down_weight[0], 1), swap(my_half(core, down_weight[0], 1, True))
    )
    hid = gate_weight.shape[2]

    def expert(x):
        sent = dot(x, w_other).astype(BF)
        sent = swap(sent)
        gu = dot(x, w_own) + sent.astype(F32)
        hidden = (jax.nn.silu(gu[:, :hid]) * gu[:, hid:]).astype(BF)
        both = jnp.concatenate([hidden, swap(hidden)], axis=1)
        return dot(both, d_both).astype(BF)

    n = routed_in.shape[0] // 2
    block_a, block_b = lax.optimization_barrier((routed_in[:n], routed_in[n:]))
    a0, b0 = along(block_a, "x"), along(block_b, "z")
    ring = {}
    for key, rows0, axis in (("a", a0, "z"), ("b", b0, "x")):
        low, high = rows0[: 2 * n], rows0[2 * n :]
        up_low = shift(low, axis, 1)
        down_high = shift(high, axis, -1)
        up_high = shift(high, axis, 1)
        down_low = shift(low, axis, -1)
        far_low = shift(up_low, axis, 1)
        far_high = shift(down_high, axis, -1)
        ring[key] = ((up_low, down_high), (up_high, down_low), (far_low, far_high))
    (a1, a2, a3), (b1, b2, b3) = ring["a"], ring["b"]
    t0 = expert(cat(a0, b0))
    t1 = expert(cat(*a1, *b1))
    t2 = expert(cat(*a2, *b2))
    last_rows, t2 = lax.optimization_barrier((cat(*a3, *b3), t2))
    t3 = expert(last_rows)
    t0, t1, t2, t3 = (t.reshape(2, 4, n, half) for t in (t0, t1, t2, t3))

    def plus(a, b):
        return (a.astype(F32) + b.astype(F32)).astype(BF)

    def sum_first(sets):
        k = n // 2
        axes = ("x", "z")
        ends = [
            (cat(*[g[3][:k] for g in groups]), cat(*[g[3][k:] for g in groups]))
            for groups in sets
        ]
        ends = lax.optimization_barrier(ends)
        got = [
            (shift(low, axis, -1), shift(high, axis, 1))
            for axis, (low, high) in zip(axes, ends)
        ]
        out = []
        for axis, groups, (low, high) in zip(axes, sets, got):
            to_down, to_up = [], []
            for i, g in enumerate(groups):
                to_down += [plus(g[1][:k], low[i * k : (i + 1) * k]), g[1][k:]]
                to_up += [g[2][:k], plus(g[2][k:], high[i * k : (i + 1) * k])]
            from_up = shift(cat(*to_down), axis, -1)
            from_down = shift(cat(*to_up), axis, 1)
            own = cat(*[g[0] for g in groups]).astype(F32)
            total = (own + from_up.astype(F32) + from_down.astype(F32)).astype(BF)
            out.append(total.reshape(len(groups), n, half))
        return out

    def sum_direct(t, axis):
        far = shift(t[3], axis, 2)
        return (
            t[0].astype(F32)
            + shift(t[1], axis, -1).astype(F32)
            + shift(t[2], axis, 1).astype(F32)
            + far.astype(F32)
        )

    sets = []
    for i in range(2):
        zero = [t0[i][o] for o in range(4)]
        minus = [t1[i][0], t1[i][1], t2[i][0], t2[i][1]]
        plus_one = [t2[i][2], t2[i][3], t1[i][2], t1[i][3]]
        sets.append([zero, minus, plus_one])
    g1 = sum_first(sets)
    g2 = [sum_direct(t3[i], axis).astype(BF) for i, axis in enumerate(("x", "z"))]
    done = []
    for i, axis in enumerate(("z", "x")):
        done.append(sum_direct((g1[i][0], g1[i][1], g1[i][2], g2[i]), axis))
    final = (stream + cat(*done)).astype(BF)

    f_keep, f_give = jnp.where(core == 0, final[:n], final[n:]), jnp.where(
        core == 0, final[n:], final[:n]
    )
    f_got = swap(f_give)
    full = jnp.concatenate(
        [jnp.where(core == 0, f_keep, f_got), jnp.where(core == 0, f_got, f_keep)], axis=1
    )
    blocks = [full[r * cap : (r + 1) * cap] for r in range(experts)]
    back = cat(blocks[0], *[shift(blocks[r], "exp", r) for r in (1, 2, 3)])
    index = ((ey - ids) % experts) * cap + rank.astype(jnp.int32)
    picking = (
        index[:, None] == jnp.arange(experts * cap, dtype=jnp.int32)[None, :]
    ).astype(BF)
    return dot(picking, back).astype(BF)


def solution(mesh):
    devices = mesh.devices
    seq, exp = devices.shape
    grid = Mesh(devices.reshape(4, seq // 8, 2, exp), SEQ + ("exp",))
    in_specs = (
        P(SEQ, "exp"),
        P(None, SEQ, "exp"),
        P(SEQ + ("exp",), None),
        P(),
        P(SEQ + ("exp",)),
        P(SEQ + ("exp",), None),
        P("exp", None),
        P("exp", None, SEQ),
        P("exp", None, SEQ),
        P("exp", SEQ, None),
    )
    out_specs = P(SEQ + ("exp",), None)
    return jax.shard_map(
        layer, mesh=grid, in_specs=in_specs, out_specs=out_specs, check_vma=False
    )
```
